1024 devices in a mesh: row: 32 (over y, x_hi), col: 32 (over x_lo, z, core).
Axes of the slice: x: 8 (x_hi: 4, x_lo: 2; x = x_hi * 2 + x_lo), y: 8, z: 8, core: 2. Of those that a mesh axis runs over, the one named last changes fastest.
Arguments:
- activations: bfloat16 [256, 8192], P('col', 'row'), may hold values from -6 to 6
- out_grad: bfloat16 [256, 8192], P('col', 'row'), may hold values from -6 to 6
- w_gate: bfloat16 [8192, 28672], P('row', 'col'), may hold values from -0.0625 to 0.0625
- w_up: bfloat16 [8192, 28672], P('row', 'col'), may hold values from -0.0625 to 0.0625
- w_down: bfloat16 [28672, 8192], P('col', 'row'), may hold values from -0.03125 to 0.03125
Outputs:
- grad_input: bfloat16 [256, 8192], P('col', 'row')
- grad_w_gate: bfloat16 [8192, 28672], P('row', 'col')
- grad_w_up: bfloat16 [8192, 28672], P('row', 'col')
- grad_w_down: bfloat16 [28672, 8192], P('col', 'row')
The draws below stay inside these ranges and needn't reach their ends.
All inputs are finite; a program needn't handle non-finite values.
Results may differ from the reference program's by a relative error of at most 0.0049.
Values may be sent and summed in bfloat16 or wider, within the bound.
A program may use at most 32 MiB of HBM per device.

```python
import jax
import jax.numpy as jnp
from jax import lax

D = 8192
FF = 28672
TOKENS = 256


def shard_levels(stream_key, extent, shards, least, high):
    def one(dim, blocks):
        steps = jax.random.uniform(jax.random.fold_in(jax.random.fold_in(stream_key, 6), dim), (blocks,), jnp.float32, least / len(shards), high / len(shards))
        return jnp.repeat(jnp.exp(steps), extent[dim] // blocks).reshape((-1,) + (1,) * (len(extent) - dim - 1))

    gain = one(*shards[0])
    for cut in shards[1:]:
        gain = gain * one(*cut)
    return gain


def noise(own_key, dims, spread, reach, pieces=(), kind=jnp.bfloat16):
    array = jax.random.normal(own_key, dims, jnp.float32) * spread
    if len(pieces) > 0:
        array = shard_levels(own_key, dims, pieces, -0.22, 0.18) * array
    return jnp.clip(array, min=-reach, max=reach).astype(kind)


def setup_inputs(seed: int = 0) -> dict:
    seeds = jax.random.split(jax.random.key(seed), 6)
    activations = noise(seeds[0], (TOKENS, D), 1.0, 6.0, ((0, 32), (1, 32)))
    out_grad = noise(seeds[1], (TOKENS, D), 1.0, 6.0, ((0, 32), (1, 32)))
    w_gate = noise(seeds[2], (D, FF), D ** -0.5, 0.0625, ((0, 32), (1, 32)))
    w_up = noise(seeds[3], (D, FF), D ** -0.5, 0.0625, ((0, 32), (1, 32)))
    w_down = noise(seeds[4], (FF, D), FF ** -0.5, 0.03125, ((0, 32), (1, 32)))
    return {"activations": activations, "out_grad": out_grad, "w_gate": w_gate, "w_up": w_up, "w_down": w_down}


def reference(activations, out_grad, w_gate, w_up, w_down):
    contract_last = (((1,), (1,)), ((), ()))
    contract_first = (((0,), (0,)), ((), ()))
    gate = jnp.dot(activations, w_gate, preferred_element_type=jnp.float32)
    upward = jnp.dot(activations, w_up, preferred_element_type=jnp.float32)
    back = lax.dot_general(out_grad, w_down, contract_last, preferred_element_type=jnp.float32)
    sigma = jax.nn.sigmoid(gate)
    hidden = (gate * sigma * upward).astype(jnp.bfloat16)
    grad_gate = (back * upward * sigma * (1.0 + gate * (1.0 - sigma))).astype(jnp.bfloat16)
    grad_up = (back * gate * sigma).astype(jnp.bfloat16)
    grad_input = lax.dot_general(grad_gate, w_gate, contract_last, preferred_element_type=jnp.float32)
    grad_input = grad_input + lax.dot_general(grad_up, w_up, contract_last, preferred_element_type=jnp.float32)
    grad_w_gate = lax.dot_general(activations, grad_gate, contract_first, preferred_element_type=jnp.float32)
    grad_w_up = lax.dot_general(activations, grad_up, contract_first, preferred_element_type=jnp.float32)
    grad_w_down = lax.dot_general(hidden, out_grad, contract_first, preferred_element_type=jnp.float32)
    return (grad_input.astype(jnp.bfloat16), grad_w_gate.astype(jnp.bfloat16), grad_w_up.astype(jnp.bfloat16), grad_w_down.astype(jnp.bfloat16))
```

```python
import functools

import jax
import jax.numpy as jnp
from jax import lax
from jax.experimental import pallas as pl
from jax.experimental.pallas import tpu as pltpu
from jax.sharding import PartitionSpec as P

MESH = pl.DeviceIdType.MESH
F32 = jnp.float32
BF16 = jnp.bfloat16

NY, NX, NZ = 8, 4, 8


def flat(value):
    n, rows, width = value.shape
    return value.astype(F32).reshape(n * rows, width).astype(BF16)


def kernel(
    act_ref, og_ref, wg_hbm, wu_hbm, wd_hbm,
    gi_ref, gwg_ref, gwu_ref, gwd_ref,
    wg, wu, wd, xbuf, tok, grd, part, rbuf, xrecv, hbuf, gpart, gsend, grecv,
    w_sem, a_send, a_recv, c_send, c_recv, x_send, x_recv, h_send, h_recv, d_send, d_recv, e_send, e_recv,
):
    row, col = lax.axis_index("row"), lax.axis_index("col")
    y, xh = row // NX, row % NX
    xl, z, core = col // (2 * NZ), (col // 2) % NZ, col % 2

    loads = [pltpu.make_async_copy(src, dst, w_sem.at[i]) for i, (src, dst) in enumerate(((wg_hbm, wg), (wu_hbm, wu), (wd_hbm, wd)))]
    for load in loads:
        load.start()

    def col_peer(slot):
        dx, dz, dc = slot // (2 * NZ), (slot // 2) % NZ, slot % 2
        peer = ((xl + dx) % 2) * (2 * NZ) + ((z + dz) % NZ) * 2 + (core + dc) % 2
        return peer, dx * (2 * NZ) + ((NZ - dz) % NZ) * 2 + dc

    def row_id(yy, xx):
        return (yy * NX + xx, col)

    barrier = pltpu.get_barrier_semaphore()

    def greet(slot, carry):
        peer, _ = col_peer(slot)
        pl.semaphore_signal(barrier, inc=1, device_id=(row, peer), device_id_type=MESH)
        return carry

    lax.fori_loop(1, 32, greet, 0)
    for t in range(NX - 1):
        pl.semaphore_signal(barrier, inc=1, device_id=row_id(y, (xh + 1 + t) % NX), device_id_type=MESH)
    for step in (1, NY - 1):
        pl.semaphore_signal(barrier, inc=1, device_id=row_id((y + step) % NY, xh), device_id_type=MESH)
    xbuf[0, 0] = act_ref[...]
    xbuf[0, 1] = og_ref[...]
    pl.semaphore_wait(barrier, 31 + (NX - 1) + 2)

    def gather_copy(slot):
        peer, there = col_peer(slot)
        return pltpu.make_async_remote_copy(
            src_ref=xbuf.at[0], dst_ref=xbuf.at[there], send_sem=a_send.at[slot], recv_sem=a_recv.at[there],
            device_id=(row, peer), device_id_type=MESH,
        )

    def gather_start(slot, carry):
        gather_copy(slot).start()
        return carry

    lax.fori_loop(1, 32, gather_start, 0)

    def gather_wait(slot, carry):
        pltpu.make_async_remote_copy(
            src_ref=xbuf.at[0], dst_ref=xbuf.at[slot], send_sem=a_send.at[slot], recv_sem=a_recv.at[slot],
            device_id=(row, col_peer(slot)[0]), device_id_type=MESH,
        ).wait()
        return carry

    lax.fori_loop(1, 32, gather_wait, 0)
    tok[...] = flat(xbuf[:, 0])
    grd[...] = flat(xbuf[:, 1])

    for load in loads:
        load.wait()
    part[:, 0] = jnp.dot(tok[...], wg[...], preferred_element_type=F32).reshape(32, 8, -1)
    part[:, 1] = jnp.dot(tok[...], wu[...], preferred_element_type=F32).reshape(32, 8, -1)
    part[:, 2] = lax.dot_general(grd[...], wd[...], (((1,), (1,)), ((), ())), preferred_element_type=F32).reshape(32, 8, -1)

    def chain(side, k, t, src):
        return pltpu.make_async_remote_copy(
            src_ref=src, dst_ref=rbuf.at[side, k - 1, t],
            send_sem=c_send.at[side, k - 1, t], recv_sem=c_recv.at[side, k - 1, t],
            device_id=row_id((y + (1 if side == 0 else NY - 1)) % NY, xh), device_id_type=MESH,
        )

    def far(side, t):
        return (t < 2) == (side == 0)

    sent = []
    for k in (4, 3, 2, 1):
        for t in range(NX):
            for side in (0, 1):
                if k == 4 and not far(side, t):
                    continue
                block = ((y + (k if side == 0 else NY - k)) % NY) * NX + (xh + 1 + t) % NX
                if k <= 2 or (k == 3 and far(side, t)):
                    held = rbuf.at[side, k, t]
                    chain(side, k + 1, t, held).wait_recv()
                    held[...] += part[block]
                    copy = chain(side, k, t, held)
                else:
                    copy = chain(side, k, t, part.at[block])
                copy.start()
                sent.append(copy)

    for t in range(NX):
        for side in (0, 1):
            chain(side, 1, t, rbuf.at[side, 0, t]).wait_recv()
        total = rbuf.at[0, 0, t]
        total[...] += rbuf[1, 0, t] + part[y * NX + (xh + 1 + t) % NX]
        if t < NX - 1:
            copy = pltpu.make_async_remote_copy(
                src_ref=total, dst_ref=xrecv.at[t], send_sem=x_send.at[t], recv_sem=x_recv.at[t],
                device_id=row_id(y, (xh + 1 + t) % NX), device_id_type=MESH,
            )
            copy.start()
            sent.append(copy)
    for t in range(NX - 1):
        pltpu.make_async_remote_copy(
            src_ref=xrecv.at[t], dst_ref=xrecv.at[t], send_sem=x_send.at[t], recv_sem=x_recv.at[t],
            device_id=row_id(y, (xh + NX - 1 - t) % NX), device_id_type=MESH,
        ).wait_recv()
    sums = rbuf[0, 0, NX - 1] + xrecv[0] + xrecv[1] + xrecv[2]
    gate, upward, back = sums[0], sums[1], sums[2]
    sigma = jax.nn.sigmoid(gate)
    mine = y * NX + xh
    hbuf[mine, 0] = (gate * sigma * upward).astype(BF16)
    hbuf[mine, 1] = (back * upward * sigma * (1.0 + gate * (1.0 - sigma))).astype(BF16)
    hbuf[mine, 2] = (back * gate * sigma).astype(BF16)

    def share(t, block):
        return pltpu.make_async_remote_copy(
            src_ref=hbuf.at[block], dst_ref=hbuf.at[block], send_sem=h_send.at[t], recv_sem=h_recv.at[t],
            device_id=row_id(y, (xh + 1 + t) % NX), device_id_type=MESH,
        )

    def forward(side, k, u, block):
        return pltpu.make_async_remote_copy(
            src_ref=hbuf.at[block], dst_ref=hbuf.at[block],
            send_sem=d_send.at[side, k - 1, u], recv_sem=d_recv.at[side, k - 1, u],
            device_id=row_id((y + (1 if side == 0 else NY - 1)) % NY, xh), device_id_type=MESH,
        )

    def source(side, k, u):
        return ((y + (NY - k if side == 0 else k)) % NY) * NX + (xh + NX - u) % NX

    for t in range(NX - 1):
        copy = share(t, mine)
        copy.start()
        sent.append(copy)
    for k in (1, 2, 3, 4):
        for u in (0, 1, 3, 2):
            if k == 1 and u > 0:
                share(u - 1, source(0, 0, u)).wait_recv()
            for side in (0, 1):
                if k == 4 and not far(side, u):
                    continue
                block = source(side, k - 1, u)
                if k > 1:
                    forward(side, k - 1, u, block).wait_recv()
                copy = forward(side, k, u, block)
                copy.start()
                sent.append(copy)
    for side in (0, 1):
        for u in range(NX):
            last = 4 if far(side, u) else 3
            forward(side, last, u, source(side, last, u)).wait_recv()

    last_dims = (((1,), (1,)), ((), ()))
    first_dims = (((0,), (0,)), ((), ()))
    grad_gate, grad_up = flat(hbuf[:, 1]), flat(hbuf[:, 2])
    gpart[...] = (
        lax.dot_general(grad_gate, wg[...], last_dims, preferred_element_type=F32)
        + lax.dot_general(grad_up, wu[...], last_dims, preferred_element_type=F32)
    ).reshape(32, 8, -1)
    gsend[...] = gpart[...].astype(BF16)

    def return_start(slot, carry):
        peer, there = col_peer(slot)
        pltpu.make_async_remote_copy(
            src_ref=gsend.at[slot], dst_ref=grecv.at[there], send_sem=e_send.at[slot], recv_sem=e_recv.at[there],
            device_id=(row, peer), device_id_type=MESH,
        ).start()
        return carry

    lax.fori_loop(1, 32, return_start, 0)
    gwg_ref[...] = lax.dot_general(tok[...], grad_gate, first_dims, preferred_element_type=F32).astype(BF16)
    gwu_ref[...] = lax.dot_general(tok[...], grad_up, first_dims, preferred_element_type=F32).astype(BF16)
    gwd_ref[...] = lax.dot_general(flat(hbuf[:, 0]), grd[...], first_dims, preferred_element_type=F32).astype(BF16)

    def return_wait(slot, total):
        pltpu.make_async_remote_copy(
            src_ref=gsend.at[slot], dst_ref=grecv.at[slot], send_sem=e_send.at[slot], recv_sem=e_recv.at[slot],
            device_id=(row, col_peer(slot)[0]), device_id_type=MESH,
        ).wait()
        return total + grecv[slot].astype(F32)

    gi_ref[...] = lax.fori_loop(1, 32, return_wait, gpart[0]).astype(BF16)
    for copy in sent:
        copy.wait_send()


def per_device(activations, out_grad, w_gate, w_up, w_down):
    depth, width = w_gate.shape
    dma = pltpu.SemaphoreType.DMA
    vmem = pl.BlockSpec(memory_space=pltpu.VMEM)
    return pl.pallas_call(
        kernel,
        out_shape=(
            jax.ShapeDtypeStruct((8, depth), BF16),
            jax.ShapeDtypeStruct((depth, width), BF16),
            jax.ShapeDtypeStruct((depth, width), BF16),
            jax.ShapeDtypeStruct((width, depth), BF16),
        ),
        in_specs=[vmem, vmem] + [pl.BlockSpec(memory_space=pl.ANY)] * 3,
        out_specs=(vmem,) * 4,
        scratch_shapes=[
            pltpu.VMEM((depth, width), BF16),
            pltpu.VMEM((depth, width), BF16),
            pltpu.VMEM((width, depth), BF16),
            pltpu.VMEM((32, 2, 8, depth), BF16),
            pltpu.VMEM((256, depth), BF16),
            pltpu.VMEM((256, depth), BF16),
            pltpu.VMEM((32, 3, 8, width), F32),
            pltpu.VMEM((2, 4, NX, 3, 8, width), F32),
            pltpu.VMEM((NX - 1, 3, 8, width), F32),
            pltpu.VMEM((32, 3, 8, width), BF16),
            pltpu.VMEM((32, 8, depth), F32),
            pltpu.VMEM((32, 8, depth), BF16),
            pltpu.VMEM((32, 8, depth), BF16),
            dma((3,)),
            dma((32,)), dma((32,)),
            dma((2, 4, NX)), dma((2, 4, NX)),
            dma((NX - 1,)), dma((NX - 1,)),
            dma((NX - 1,)), dma((NX - 1,)),
            dma((2, 4, NX)), dma((2, 4, NX)),
            dma((32,)), dma((32,)),
        ],
        compiler_params=pltpu.CompilerParams(collective_id=0, has_side_effects=True, vmem_limit_bytes=48 << 20),
        name="ffn_backward",
    )(activations, out_grad, w_gate, w_up, w_down)


def solution(mesh):
    in_specs = (P("col", "row"), P("col", "row"), P("row", "col"), P("row", "col"), P("col", "row"))
    out_specs = (P("col", "row"), P("row", "col"), P("row", "col"), P("col", "row"))
    return jax.shard_map(
        per_device, mesh=mesh, in_specs=in_specs, out_specs=out_specs, check_vma=False
    )
```

```python
import functools

import jax
import jax.numpy as jnp
from jax import lax
from jax.experimental import pallas as pl
from jax.experimental.pallas import tpu as pltpu
from jax.sharding import PartitionSpec as P

MESH = pl.DeviceIdType.MESH
F32 = jnp.float32
BF16 = jnp.bfloat16

NY, NX, NZ = 8, 4, 8
LAST_DIMS = (((1,), (1,)), ((), ()))
FIRST_DIMS = (((0,), (0,)), ((), ()))


def flat(value):
    n, rows, width = value.shape
    return value.astype(F32).reshape(n * rows, width).astype(BF16)


def far(side, t):
    return (t < 2) == (side == 0)


def narrow(side, k, t):
    return k >= 3 or (k == 2 and not far(side, t))


def kernel(
    bounds,
    act_hbm, og_hbm, wg_hbm, wu_hbm, wd_hbm,
    gi_hbm, gwg_hbm, gwu_hbm, gwd_hbm,
    gi_ref, gwg_ref, gwu_ref, gwd_ref, wg, wu, wd, xbuf, tok, grd, gpart, gcore, gcore_in, gline, gline_in, gown, gown_in,
    w_sem, o_sem, a_send, a_recv, c_send, c_recv, x_send, x_recv, h_send, h_recv, d_send, d_recv, e_send, e_recv,
    *parts,
):
    row, col = lax.axis_index("row"), lax.axis_index("col")
    y, xh = row // NX, row % NX
    xl, z, core = col // (2 * NZ), (col // 2) % NZ, col % 2
    mine = y * NX + xh
    halves = [parts[7 * h : 7 * h + 7] for h in range(len(bounds))]

    def col_id(dx, dz, dc):
        return (row, ((xl + dx) % 2) * (2 * NZ) + ((z + dz) % NZ) * 2 + (core + dc) % 2)

    def row_id(dy, dx):
        return (((y + dy) % NY) * NX + (xh + dx) % NX, col)

    sent = []

    def remote(src, dst, send, recv, device, start=True):
        copy = pltpu.make_async_remote_copy(
            src_ref=src, dst_ref=dst, send_sem=send, recv_sem=recv, device_id=device, device_id_type=MESH
        )
        if start:
            copy.start()
            sent.append(copy)
        return copy

    own = [
        pltpu.make_async_copy(act_hbm, xbuf.at[0, 0], w_sem.at[0]),
        pltpu.make_async_copy(og_hbm, xbuf.at[0, 1], w_sem.at[1]),
    ]
    loads = [
        pltpu.make_async_copy(src, dst, w_sem.at[2 + i])
        for i, (src, dst) in enumerate(((wg_hbm, wg), (wu_hbm, wu), (wd_hbm, wd)))
    ]
    for load in own + loads:
        load.start()

    barrier = pltpu.get_barrier_semaphore()
    partners = [col_id(0, dz, 0) for dz in range(1, NZ)] + [col_id(1, 0, 0), col_id(0, 0, 1)]
    partners += [row_id(1, 0), row_id(NY - 1, 0)] + [row_id(0, dx) for dx in range(1, NX)]
    for partner in partners:
        pl.semaphore_signal(barrier, inc=1, device_id=partner, device_id_type=MESH)
    for load in own:
        load.wait()
    pl.semaphore_wait(barrier, len(partners))

    def gather(slot, there, device, start=True):
        return remote(xbuf.at[slot], xbuf.at[there], a_send.at[there], a_recv.at[there], device, start)

    def arrived(slot):
        gather(slot, slot, col_id(0, 0, 1), start=False).wait_recv()

    def to_core(slot):
        gather(slot, slot + 1, col_id(0, 0, 1))

    order = (1, 7, 2, 6, 3, 5, 4)
    for dz in order:
        gather(0, (NZ - dz) * 2, col_id(0, dz, 0))
    gather(0, 2 * NZ, col_id(1, 0, 0))
    to_core(0)
    for dz in order:
        arrived(2 * dz)
        gather(2 * dz, 2 * NZ + 2 * dz, col_id(1, 0, 0))
        to_core(2 * dz)
    for dz in (0,) + order:
        arrived(2 * NZ + 2 * dz)
        to_core(2 * NZ + 2 * dz)
    for slot in range(1, 32, 2):
        arrived(slot)
    tok[...] = flat(xbuf[:, 0])
    grd[...] = flat(xbuf[:, 1])
    for load in loads:
        load.wait()

    def products(h):
        low, high = bounds[h]
        part = halves[h][0]
        part[:, 0] = jnp.dot(tok[...], wg[:, low:high], preferred_element_type=F32).reshape(32, 8, high - low)
        part[:, 1] = jnp.dot(tok[...], wu[:, low:high], preferred_element_type=F32).reshape(32, 8, high - low)
        part[:, 2] = lax.dot_general(
            grd[...], wd[low:high, :], LAST_DIMS, preferred_element_type=F32
        ).reshape(32, 8, high - low)

    def chain_in(h, side, k, t):
        _, _, in16, _, in32, _, _ = halves[h]
        return in16.at[side, k - 2, t] if narrow(side, k, t) else in32.at[side, k - 1, t]

    def chain(h, side, k, t, start=True):
        _, out16, _, out32, _, _, _ = halves[h]
        out = out16.at[side, k - 2, t] if narrow(side, k, t) else out32.at[side, k - 1, t]
        return remote(
            out, chain_in(h, side, k, t), c_send.at[h, side, k - 1, t], c_recv.at[h, side, k - 1, t],
            row_id(1 if side == 0 else NY - 1, 0), start,
        )

    def hop(h, k, near=True, distant=True):
        part, out16, _, out32, _, _, _ = halves[h]
        order = [(side, t) for t in range(NX) for side in (0, 1)]
        if k > 1:
            order = [p for p in order if not far(*p)] + [p for p in order if far(*p)]
        for side, t in order:
            if (k == 4 and not far(side, t)) or not (distant if far(side, t) else near):
                continue
            block = ((y + (k if side == 0 else NY - k)) % NY) * NX + (xh + 1 + t) % NX
            value = part[block]
            if k <= 2 or (k == 3 and far(side, t)):
                chain(h, side, k + 1, t, start=False).wait_recv()
                value += chain_in(h, side, k + 1, t)[...].astype(F32)
            if narrow(side, k, t):
                out16[side, k - 2, t] = value.astype(BF16)
            else:
                out32[side, k - 1, t] = value
            chain(h, side, k, t)

    def cross(h, t, there, start=True):
        _, _, _, out32, _, xin, _ = halves[h]
        return remote(
            xin.at[0, t], xin.at[1, t], x_send.at[h, t], x_recv.at[h, t], row_id(0, there), start
        )

    def turn(h):
        part, _, _, _, in32, xin, _ = halves[h]
        for t in range(NX):
            for side in (0, 1):
                chain(h, side, 1, t, start=False).wait_recv()
            xin[0, t] = in32[0, 0, t] + in32[1, 0, t] + part[y * NX + (xh + 1 + t) % NX]
            if t < NX - 1:
                cross(h, t, 1 + t)

    def share(h, t, block, start=True):
        hbuf = halves[h][6]
        return remote(
            hbuf.at[block], hbuf.at[block], h_send.at[h, t], h_recv.at[h, t], row_id(0, 1 + t), start
        )

    def forward(h, side, k, u, block, start=True):
        hbuf = halves[h][6]
        return remote(
            hbuf.at[block], hbuf.at[block], d_send.at[h, side, k - 1, u], d_recv.at[h, side, k - 1, u],
            row_id(1 if side == 0 else NY - 1, 0), start,
        )

    def source(side, k, u):
        return ((y + (NY - k if side == 0 else k)) % NY) * NX + (xh + NX - u) % NX

    def activate(h):
        _, _, _, _, _, xin, hbuf = halves[h]
        for t in (0, 2, 1):
            cross(h, t, 1 + t, start=False).wait_recv()
        sums = xin[0, NX - 1] + xin[1, 0] + xin[1, 1] + xin[1, 2]
        gate, upward, back = sums[0], sums[1], sums[2]
        sigma = jax.nn.sigmoid(gate)
        hbuf[mine, 0] = (gate * sigma * upward).astype(BF16)
        hbuf[mine, 1] = (back * upward * sigma * (1.0 + gate * (1.0 - sigma))).astype(BF16)
        hbuf[mine, 2] = (back * gate * sigma).astype(BF16)
        for side in (0, 1):
            forward(h, side, 1, 0, mine)
        for t in (0, 2, 1):
            share(h, t, mine)

    def spread(h, k):
        for u in (0, 1, 3, 2):
            if k == 1 and u == 0:
                continue
            if k == 1:
                share(h, u - 1, source(0, 0, u), start=False).wait_recv()
            for side in (0, 1):
                if k == 4 and not far(side, u):
                    continue
                block = source(side, k - 1, u)
                if k > 1:
                    forward(h, side, k - 1, u, block, start=False).wait_recv()
                forward(h, side, k, u, block)

    def landed(h):
        for u in (0, 1, 3, 2):
            for side in (0, 1):
                last = 4 if far(side, u) else 3
                forward(h, side, last, u, source(side, last, u), start=False).wait_recv()

    products(0)
    hop(0, 4)
    hop(0, 3, distant=False)
    products(1)
    hop(0, 3, near=False)
    hop(1, 4)
    hop(0, 2)
    hop(1, 3)
    hop(0, 1)
    hop(1, 2)
    turn(0)
    hop(1, 1)
    activate(0)
    turn(1)
    spread(0, 1)
    spread(0, 2)
    activate(1)
    spread(0, 3)
    spread(1, 1)
    spread(0, 4)
    spread(1, 2)
    spread(1, 3)
    spread(1, 4)
    landed(0)
    landed(1)

    def store(i):
        refs = ((gi_ref, gi_hbm), (gwg_ref, gwg_hbm), (gwu_ref, gwu_hbm), (gwd_ref, gwd_hbm))[i]
        copy = pltpu.make_async_copy(*refs, o_sem.at[i])
        copy.start()
        return copy

    grads = [(flat(half[6][:, 1]), flat(half[6][:, 2])) for half in halves]
    total = None
    for (low, high), (grad_gate, grad_up) in zip(bounds, grads):
        for grad, weight in ((grad_gate, wg), (grad_up, wu)):
            term = lax.dot_general(grad, weight[:, low:high], LAST_DIMS, preferred_element_type=F32)
            total = term if total is None else total + term
    total = total.reshape(16, 2, 8, total.shape[1])
    gpart[...] = total[:, 0]
    gcore[...] = total[:, 1]
    step = remote(gcore, gcore_in, e_send.at[8], e_recv.at[8], col_id(0, 0, 1))
    for (low, high), (grad_gate, _) in zip(bounds, grads):
        gwg_ref[:, low:high] = lax.dot_general(
            tok[...], grad_gate, FIRST_DIMS, preferred_element_type=F32
        ).astype(BF16)
    stored = [store(1)]
    step.wait_recv()
    gline[...] = gpart[NZ:] + gcore_in[NZ:]
    step = remote(gline, gline_in, e_send.at[9], e_recv.at[9], col_id(1, 0, 0))
    for (low, high), (_, grad_up) in zip(bounds, grads):
        gwu_ref[:, low:high] = lax.dot_general(
            tok[...], grad_up, FIRST_DIMS, preferred_element_type=F32
        ).astype(BF16)
    stored.append(store(2))
    step.wait_recv()
    gown[...] = gpart[:NZ] + gcore_in[:NZ] + gline_in[...]
    for dz in order:
        remote(gown.at[dz], gown_in.at[NZ - dz], e_send.at[NZ - dz], e_recv.at[NZ - dz], col_id(0, dz, 0))
    for (low, high), half in zip(bounds, halves):
        gwd_ref[low:high, :] = lax.dot_general(
            flat(half[6][:, 0]), grd[...], FIRST_DIMS, preferred_element_type=F32
        ).astype(BF16)
    stored.append(store(3))
    result = gown[0]
    for dz in order:
        remote(gown.at[dz], gown_in.at[dz], e_send.at[dz], e_recv.at[dz], col_id(0, dz, 0), start=False).wait_recv()
        result += gown_in[dz]
    gi_ref[...] = result.astype(BF16)
    stored.append(store(0))
    for copy in sent:
        copy.wait_send()
    for copy in stored:
        copy.wait()


def deliver(*refs):
    sources, targets, sems = refs[:4], refs[4:8], refs[8]
    copies = [pltpu.make_async_copy(s, t, sems.at[i]) for i, (s, t) in enumerate(zip(sources, targets))]
    for copy in copies:
        copy.start()
    for copy in copies:
        copy.wait()


def per_device(activations, out_grad, w_gate, w_up, w_down):
    depth, width = w_gate.shape
    cut = (width // 128 + 1) // 2 * 128
    bounds = ((0, cut), (cut, width))
    dma = pltpu.SemaphoreType.DMA
    hbm = pl.BlockSpec(memory_space=pltpu.MemorySpace.HBM)
    shapes = (
        jax.ShapeDtypeStruct((8, depth), BF16),
        jax.ShapeDtypeStruct((depth, width), BF16),
        jax.ShapeDtypeStruct((depth, width), BF16),
        jax.ShapeDtypeStruct((width, depth), BF16),
    )
    parts = []
    for low, high in bounds:
        block = (3, 8, high - low)
        parts += [
            pltpu.VMEM((32,) + block, F32),
            pltpu.VMEM((2, 3, NX) + block, BF16),
            pltpu.VMEM((2, 3, NX) + block, BF16),
            pltpu.VMEM((2, 2, NX) + block, F32),
            pltpu.VMEM((2, 2, NX) + block, F32),
            pltpu.VMEM((2, NX) + block, F32),
            pltpu.VMEM((32,) + block, BF16),
        ]
    n = len(bounds)
    results = pl.pallas_call(
        functools.partial(kernel, bounds),
        out_shape=shapes,
        in_specs=[hbm] * 5,
        out_specs=(hbm,) * 4,
        scratch_shapes=[pltpu.VMEM(shape.shape, BF16) for shape in shapes]
        + [
            pltpu.VMEM((depth, width), BF16),
            pltpu.VMEM((depth, width), BF16),
            pltpu.VMEM((width, depth), BF16),
            pltpu.VMEM((32, 2, 8, depth), BF16),
            pltpu.VMEM((256, depth), BF16),
            pltpu.VMEM((256, depth), BF16),
            pltpu.VMEM((16, 8, depth), F32),
            pltpu.VMEM((16, 8, depth), F32),
            pltpu.VMEM((16, 8, depth), F32),
            pltpu.VMEM((NZ, 8, depth), F32),
            pltpu.VMEM((NZ, 8, depth), F32),
            pltpu.VMEM((NZ, 8, depth), F32),
            pltpu.VMEM((NZ, 8, depth), F32),
            dma((5,)), dma((4,)),
            dma((32,)), dma((32,)),
            dma((n, 2, 4, NX)), dma((n, 2, 4, NX)),
            dma((n, NX - 1)), dma((n, NX - 1)),
            dma((n, NX - 1)), dma((n, NX - 1)),
            dma((n, 2, 4, NX)), dma((n, 2, 4, NX)),
            dma((10,)), dma((10,)),
        ] + parts,
        compiler_params=pltpu.CompilerParams(collective_id=0, has_side_effects=True, vmem_limit_bytes=60 << 20),
        name="ffn_backward",
    )(activations, out_grad, w_gate, w_up, w_down)
    return pl.pallas_call(
        deliver,
        out_shape=shapes,
        in_specs=[hbm] * 4,
        out_specs=(hbm,) * 4,
        scratch_shapes=[dma((4,))],
        name="deliver",
    )(*results)


def solution(mesh):
    in_specs = (P("col", "row"), P("col", "row"), P("row", "col"), P("row", "col"), P("col", "row"))
    out_specs = (P("col", "row"), P("row", "col"), P("row", "col"), P("col", "row"))
    return jax.shard_map(
        per_device, mesh=mesh, in_specs=in_specs, out_specs=out_specs, check_vma=False
    )
```

```python
import functools

import jax
import jax.numpy as jnp
from jax import lax
from jax.experimental import pallas as pl
from jax.experimental.pallas import tpu as pltpu
from jax.sharding import PartitionSpec as P

MESH = pl.DeviceIdType.MESH
F32 = jnp.float32
BF16 = jnp.bfloat16

NY, NX, NZ = 8, 4, 8
LAST_DIMS = (((1,), (1,)), ((), ()))
FIRST_DIMS = (((0,), (0,)), ((), ()))


def flat(value):
    n, rows, width = value.shape
    return value.astype(F32).reshape(n * rows, width).astype(BF16)


def far(side, t):
    return (t < 2) == (side == 0)


def narrow(side, k, t):
    return k >= 3 or (k == 2 and not far(side, t))


def kernel(
    bounds,
    act_hbm, og_hbm, wg_hbm, wu_hbm, wd_hbm,
    gi_ref, gwg_ref, gwu_ref, gwd_ref,
    wg, wu, wd, xbuf, tok, grd, gpart, gsend, grecv,
    w_sem, a_send, a_recv, c_send, c_recv, x_send, x_recv, h_send, h_recv, d_send, d_recv, e_send, e_recv,
    *parts,
):
    row, col = lax.axis_index("row"), lax.axis_index("col")
    y, xh = row // NX, row % NX
    xl, z, core = col // (2 * NZ), (col // 2) % NZ, col % 2
    mine = y * NX + xh
    halves = [parts[7 * h : 7 * h + 7] for h in range(len(bounds))]

    def col_id(dx, dz, dc):
        return (row, ((xl + dx) % 2) * (2 * NZ) + ((z + dz) % NZ) * 2 + (core + dc) % 2)

    def slot_id(slot):
        return col_id(slot // (2 * NZ), (slot // 2) % NZ, slot % 2)

    def slot_there(slot):
        return slot // (2 * NZ) * (2 * NZ) + (NZ - (slot // 2) % NZ) % NZ * 2 + slot % 2

    def row_id(dy, dx):
        return (((y + dy) % NY) * NX + (xh + dx) % NX, col)

    sent = []

    def remote(src, dst, send, recv, device, start=True):
        copy = pltpu.make_async_remote_copy(
            src_ref=src, dst_ref=dst, send_sem=send, recv_sem=recv, device_id=device, device_id_type=MESH
        )
        if start:
            copy.start()
            sent.append(copy)
        return copy

    own = [
        pltpu.make_async_copy(act_hbm, xbuf.at[0, 0], w_sem.at[0]),
        pltpu.make_async_copy(og_hbm, xbuf.at[0, 1], w_sem.at[1]),
    ]
    loads = [
        pltpu.make_async_copy(src, dst, w_sem.at[2 + i])
        for i, (src, dst) in enumerate(((wg_hbm, wg), (wu_hbm, wu), (wd_hbm, wd)))
    ]
    for load in own + loads:
        load.start()

    barrier = pltpu.get_barrier_semaphore()

    def greet(slot, carry):
        pl.semaphore_signal(barrier, inc=1, device_id=slot_id(slot), device_id_type=MESH)
        return carry

    lax.fori_loop(1, 32, greet, 0)
    partners = [row_id(1, 0), row_id(NY - 1, 0)] + [row_id(0, dx) for dx in range(1, NX)]
    for partner in partners:
        pl.semaphore_signal(barrier, inc=1, device_id=partner, device_id_type=MESH)
    for load in own:
        load.wait()
    pl.semaphore_wait(barrier, 31 + len(partners))

    def gather(slot, there, device, start=True):
        return remote(xbuf.at[slot], xbuf.at[there], a_send.at[there], a_recv.at[there], device, start)

    order = [dx * 2 * NZ + dz * 2 for dz in (0, 1, 7, 2, 6, 3, 5, 4) for dx in (0, 1)]
    for slot in order[1:]:
        gather(0, slot_there(slot), slot_id(slot))
    for slot in order:
        if slot > 0:
            gather(slot, slot, slot_id(1), start=False).wait_recv()
        gather(slot, slot + 1, slot_id(1))
    for slot in order:
        gather(slot + 1, slot + 1, slot_id(1), start=False).wait_recv()
    tok[...] = flat(xbuf[:, 0])
    grd[...] = flat(xbuf[:, 1])
    for load in loads:
        load.wait()

    def products(h):
        low, high = bounds[h]
        part = halves[h][0]
        part[:, 0] = jnp.dot(tok[...], wg[:, low:high], preferred_element_type=F32).reshape(32, 8, high - low)
        part[:, 1] = jnp.dot(tok[...], wu[:, low:high], preferred_element_type=F32).reshape(32, 8, high - low)
        part[:, 2] = lax.dot_general(
            grd[...], wd[low:high, :], LAST_DIMS, preferred_element_type=F32
        ).reshape(32, 8, high - low)

    def chain_in(h, side, k, t):
        _, _, in16, _, in32, _, _ = halves[h]
        return in16.at[side, k - 2, t] if narrow(side, k, t) else in32.at[side, k - 1, t]

    def chain(h, side, k, t, start=True):
        _, out16, _, out32, _, _, _ = halves[h]
        out = out16.at[side, k - 2, t] if narrow(side, k, t) else out32.at[side, k - 1, t]
        return remote(
            out, chain_in(h, side, k, t), c_send.at[h, side, k - 1, t], c_recv.at[h, side, k - 1, t],
            row_id(1 if side == 0 else NY - 1, 0), start,
        )

    def hop(h, k, near=True, distant=True):
        part, out16, _, out32, _, _, _ = halves[h]
        order = [(side, t) for t in range(NX) for side in (0, 1)]
        if k > 1:
            order = [p for p in order if not far(*p)] + [p for p in order if far(*p)]
        for side, t in order:
            if (k == 4 and not far(side, t)) or not (distant if far(side, t) else near):
                continue
            block = ((y + (k if side == 0 else NY - k)) % NY) * NX + (xh + 1 + t) % NX
            value = part[block]
            if k <= 2 or (k == 3 and far(side, t)):
                chain(h, side, k + 1, t, start=False).wait_recv()
                value += chain_in(h, side, k + 1, t)[...].astype(F32)
            if narrow(side, k, t):
                out16[side, k - 2, t] = value.astype(BF16)
            else:
                out32[side, k - 1, t] = value
            chain(h, side, k, t)

    def cross(h, t, there, start=True):
        _, _, _, out32, _, xin, _ = halves[h]
        return remote(
            xin.at[0, t], xin.at[1, t], x_send.at[h, t], x_recv.at[h, t], row_id(0, there), start
        )

    def turn(h):
        part, _, _, _, in32, xin, _ = halves[h]
        for t in range(NX):
            for side in (0, 1):
                chain(h, side, 1, t, start=False).wait_recv()
            xin[0, t] = in32[0, 0, t] + in32[1, 0, t] + part[y * NX + (xh + 1 + t) % NX]
            if t < NX - 1:
                cross(h, t, 1 + t)

    def share(h, t, block, start=True):
        hbuf = halves[h][6]
        return remote(
            hbuf.at[block], hbuf.at[block], h_send.at[h, t], h_recv.at[h, t], row_id(0, 1 + t), start
        )

    def forward(h, side, k, u, block, start=True):
        hbuf = halves[h][6]
        return remote(
            hbuf.at[block], hbuf.at[block], d_send.at[h, side, k - 1, u], d_recv.at[h, side, k - 1, u],
            row_id(1 if side == 0 else NY - 1, 0), start,
        )

    def source(side, k, u):
        return ((y + (NY - k if side == 0 else k)) % NY) * NX + (xh + NX - u) % NX

    def activate(h):
        _, _, _, _, _, xin, hbuf = halves[h]
        for t in (0, 2, 1):
            cross(h, t, 1 + t, start=False).wait_recv()
        sums = xin[0, NX - 1] + xin[1, 0] + xin[1, 1] + xin[1, 2]
        gate, upward, back = sums[0], sums[1], sums[2]
        sigma = jax.nn.sigmoid(gate)
        hbuf[mine, 0] = (gate * sigma * upward).astype(BF16)
        hbuf[mine, 1] = (back * upward * sigma * (1.0 + gate * (1.0 - sigma))).astype(BF16)
        hbuf[mine, 2] = (back * gate * sigma).astype(BF16)
        for side in (0, 1):
            forward(h, side, 1, 0, mine)
        for t in (0, 2, 1):
            share(h, t, mine)

    def spread(h, k):
        for u in (0, 1, 3, 2):
            if k == 1 and u == 0:
                continue
            if k == 1:
                share(h, u - 1, source(0, 0, u), start=False).wait_recv()
            for side in (0, 1):
                if k == 4 and not far(side, u):
                    continue
                block = source(side, k - 1, u)
                if k > 1:
                    forward(h, side, k - 1, u, block, start=False).wait_recv()
                forward(h, side, k, u, block)

    def landed(h):
        for u in (0, 1, 3, 2):
            for side in (0, 1):
                last = 4 if far(side, u) else 3
                forward(h, side, last, u, source(side, last, u), start=False).wait_recv()

    products(0)
    hop(0, 4)
    hop(0, 3, distant=False)
    products(1)
    hop(0, 3, near=False)
    hop(1, 4)
    hop(0, 2)
    hop(1, 3)
    hop(0, 1)
    hop(1, 2)
    turn(0)
    hop(1, 1)
    activate(0)
    turn(1)
    spread(0, 1)
    spread(0, 2)
    activate(1)
    spread(0, 3)
    spread(1, 1)
    spread(0, 4)
    spread(1, 2)
    spread(1, 3)
    spread(1, 4)
    landed(0)
    landed(1)

    grads = [(flat(half[6][:, 1]), flat(half[6][:, 2])) for half in halves]
    total = None
    for (low, high), (grad_gate, grad_up) in zip(bounds, grads):
        for grad, weight in ((grad_gate, wg), (grad_up, wu)):
            term = lax.dot_general(grad, weight[:, low:high], LAST_DIMS, preferred_element_type=F32)
            total = term if total is None else total + term
    gpart[...] = total.reshape(32, 8, total.shape[1])
    gsend[...] = gpart[...].astype(BF16)

    def returned(slot, there, device):
        return pltpu.make_async_remote_copy(
            src_ref=gsend.at[slot], dst_ref=grecv.at[there], send_sem=e_send.at[slot], recv_sem=e_recv.at[there],
            device_id=device, device_id_type=MESH,
        )

    def return_start(slot, carry):
        returned(slot, slot_there(slot), slot_id(slot)).start()
        return carry

    lax.fori_loop(1, 32, return_start, 0)
    for (low, high), half, (grad_gate, grad_up) in zip(bounds, halves, grads):
        for out, grad in ((gwg_ref, grad_gate), (gwu_ref, grad_up)):
            out[:, low:high] = lax.dot_general(
                tok[...], grad, FIRST_DIMS, preferred_element_type=F32
            ).astype(BF16)
        gwd_ref[low:high, :] = lax.dot_general(
            flat(half[6][:, 0]), grd[...], FIRST_DIMS, preferred_element_type=F32
        ).astype(BF16)
    for copy in sent:
        copy.wait_send()

    def return_wait(slot, carry):
        returned(slot, slot, slot_id(slot)).wait()
        return carry

    lax.fori_loop(1, 32, return_wait, 0)
    gi_ref[...] = (gpart[0] + jnp.sum(grecv[1:].astype(F32), axis=0)).astype(BF16)


def deliver(*refs):
    sources, targets, sems = refs[:4], refs[4:8], refs[8]
    copies = [pltpu.make_async_copy(s, t, sems.at[i]) for i, (s, t) in enumerate(zip(sources, targets))]
    for copy in copies:
        copy.start()
    for copy in copies:
        copy.wait()


def per_device(activations, out_grad, w_gate, w_up, w_down):
    depth, width = w_gate.shape
    cut = (width // 128 + 1) // 2 * 128
    bounds = ((0, cut), (cut, width))
    dma = pltpu.SemaphoreType.DMA
    vmem = pl.BlockSpec(memory_space=pltpu.VMEM)
    hbm = pl.BlockSpec(memory_space=pltpu.MemorySpace.HBM)
    shapes = (
        jax.ShapeDtypeStruct((8, depth), BF16),
        jax.ShapeDtypeStruct((depth, width), BF16),
        jax.ShapeDtypeStruct((depth, width), BF16),
        jax.ShapeDtypeStruct((width, depth), BF16),
    )
    parts = []
    for low, high in bounds:
        block = (3, 8, high - low)
        parts += [
            pltpu.VMEM((32,) + block, F32),
            pltpu.VMEM((2, 3, NX) + block, BF16),
            pltpu.VMEM((2, 3, NX) + block, BF16),
            pltpu.VMEM((2, 2, NX) + block, F32),
            pltpu.VMEM((2, 2, NX) + block, F32),
            pltpu.VMEM((2, NX) + block, F32),
            pltpu.VMEM((32,) + block, BF16),
        ]
    n = len(bounds)
    operands = [pltpu.with_memory_space_constraint(x, pltpu.MemorySpace.HBM) for x in (activations, out_grad, w_gate, w_up, w_down)]
    results = pl.pallas_call(
        functools.partial(kernel, bounds),
        out_shape=tuple(pltpu.VMEM(shape.shape, BF16) for shape in shapes),
        in_specs=[hbm] * 5,
        out_specs=(vmem,) * 4,
        scratch_shapes=[
            pltpu.VMEM((depth, width), BF16),
            pltpu.VMEM((depth, width), BF16),
            pltpu.VMEM((width, depth), BF16),
            pltpu.VMEM((32, 2, 8, depth), BF16),
            pltpu.VMEM((256, depth), BF16),
            pltpu.VMEM((256, depth), BF16),
            pltpu.VMEM((32, 8, depth), F32),
            pltpu.VMEM((32, 8, depth), BF16),
            pltpu.VMEM((32, 8, depth), BF16),
            dma((5,)),
            dma((32,)), dma((32,)),
            dma((n, 2, 4, NX)), dma((n, 2, 4, NX)),
            dma((n, NX - 1)), dma((n, NX - 1)),
            dma((n, NX - 1)), dma((n, NX - 1)),
            dma((n, 2, 4, NX)), dma((n, 2, 4, NX)),
            dma((32,)), dma((32,)),
        ] + parts,
        compiler_params=pltpu.CompilerParams(collective_id=0, has_side_effects=True, vmem_limit_bytes=60 << 20),
        name="ffn_backward",
    )(*operands)
    return pl.pallas_call(
        deliver,
        out_shape=shapes,
        in_specs=[vmem] * 4,
        out_specs=(hbm,) * 4,
        scratch_shapes=[dma((4,))],
        compiler_params=pltpu.CompilerParams(vmem_limit_bytes=4 << 20),
        name="deliver",
    )(*results)


def solution(mesh):
    in_specs = (P("col", "row"), P("col", "row"), P("row", "col"), P("row", "col"), P("col", "row"))
    out_specs = (P("col", "row"), P("row", "col"), P("row", "col"), P("col", "row"))
    return jax.shard_map(
        per_device, mesh=mesh, in_specs=in_specs, out_specs=out_specs, check_vma=False
    )
```

```python
import functools

import jax
import jax.numpy as jnp
from jax import lax
from jax.experimental import pallas as pl
from jax.experimental.pallas import tpu as pltpu
from jax.sharding import PartitionSpec as P

MESH = pl.DeviceIdType.MESH
F32 = jnp.float32
BF16 = jnp.bfloat16

NY, NX, NZ = 8, 4, 8
FIRST, LATER = (4, 3, 5), (2, 6, 1, 7, 0)
LAST_DIMS = (((1,), (1,)), ((), ()))
FIRST_DIMS = (((0,), (0,)), ((), ()))


ORDER = (
    (0, 1, 4, 0, 0), (0, 1, 4, 0, 1), (0, 1, 4, 1, 2), (0, 1, 4, 1, 3), (0, 1, 3, 0, 2), (0, 1, 3, 0, 3),
    (0, 1, 3, 1, 0), (0, 1, 3, 1, 1), (0, 0, 4, 0, 0), (0, 0, 4, 0, 1), (0, 0, 4, 1, 2), (0, 0, 4, 1, 3),
    (0, 0, 3, 0, 2), (0, 0, 3, 0, 3), (0, 1, 3, 0, 0), (0, 1, 3, 0, 1), (0, 1, 3, 1, 2), (0, 1, 3, 1, 3),
    (0, 0, 3, 1, 0), (0, 0, 3, 1, 1), (0, 2, 4, 0, 0), (0, 2, 4, 0, 1), (0, 0, 3, 0, 0), (4, 0), (0, 1, 2, 0, 2),
    (0, 1, 2, 0, 3), (0, 1, 2, 1, 0), (0, 1, 2, 1, 1), (0, 1, 2, 1, 2), (0, 1, 2, 0, 0), (0, 1, 2, 1, 3),
    (0, 1, 2, 0, 1), (0, 0, 3, 1, 2), (0, 0, 3, 0, 1), (0, 0, 3, 1, 3), (0, 2, 4, 1, 2), (0, 2, 4, 1, 3),
    (0, 0, 2, 0, 2), (0, 1, 1, 0, 2), (0, 1, 1, 0, 3), (0, 1, 1, 1, 0), (0, 1, 1, 1, 1), (0, 0, 2, 0, 3),
    (0, 0, 2, 1, 0), (0, 1, 1, 0, 0), (0, 1, 1, 1, 2), (0, 0, 2, 1, 1), (0, 1, 1, 0, 1), (0, 1, 1, 1, 3),
    (0, 0, 2, 0, 0), (0, 0, 2, 0, 1), (0, 0, 2, 1, 2), (0, 0, 2, 1, 3), (0, 2, 3, 0, 2), (0, 2, 3, 0, 3),
    (0, 2, 3, 1, 0), (0, 2, 3, 1, 1), (0, 2, 3, 0, 0), (0, 2, 3, 0, 1), (0, 2, 3, 1, 2), (0, 2, 3, 1, 3),
    (0, 0, 1, 0, 2), (0, 0, 1, 0, 3), (1, 1, 0), (0, 0, 1, 1, 0), (1, 1, 1), (1, 1, 2), (0, 0, 1, 1, 1),
    (0, 0, 1, 0, 0), (1, 1, 3), (0, 0, 1, 0, 1), (0, 0, 1, 1, 2), (0, 2, 2, 0, 2), (0, 2, 2, 0, 3), (0, 2, 2, 0, 0),
    (0, 0, 1, 1, 3), (0, 2, 2, 0, 1), (0, 2, 2, 1, 0), (0, 2, 2, 1, 1), (0, 2, 2, 1, 2), (0, 2, 2, 1, 3), (2, 1),
    (1, 0, 0), (1, 0, 1), (1, 0, 2), (0, 2, 1, 0, 2), (0, 2, 1, 0, 3), (1, 0, 3), (0, 2, 1, 0, 0), (0, 2, 1, 1, 0),
    (0, 2, 1, 1, 1), (0, 2, 1, 0, 1), (3, 1, 2, 0, 0), (0, 2, 1, 1, 2), (3, 1, 2, 0, 1), (3, 1, 2, 0, 3),
    (0, 2, 1, 1, 3), (3, 1, 2, 0, 2), (3, 1, 2, 1, 0), (3, 1, 2, 1, 1), (3, 1, 2, 1, 3), (3, 1, 2, 1, 2), (1, 2, 0),
    (1, 2, 1), (3, 1, 3, 0, 0), (1, 2, 2), (3, 1, 3, 0, 1), (2, 0), (3, 1, 3, 0, 3), (3, 1, 3, 0, 2), (3, 1, 3, 1, 0),
    (3, 1, 3, 1, 1), (3, 1, 3, 1, 3), (1, 2, 3), (3, 1, 3, 1, 2), (3, 1, 4, 0, 0), (3, 1, 4, 0, 1), (3, 0, 2, 0, 0),
    (3, 0, 2, 1, 0), (3, 0, 2, 0, 1), (3, 0, 2, 1, 1), (2, 2), (3, 0, 2, 0, 3), (3, 0, 2, 1, 3), (3, 0, 2, 0, 2),
    (3, 0, 2, 1, 2), (3, 1, 4, 1, 3), (3, 1, 4, 1, 2), (3, 0, 3, 0, 0), (3, 0, 3, 1, 0), (3, 0, 3, 0, 1),
    (3, 0, 3, 1, 1), (3, 2, 2, 0, 0), (3, 2, 2, 1, 0), (3, 2, 2, 0, 1), (3, 2, 2, 1, 1), (3, 2, 2, 0, 3),
    (3, 2, 2, 1, 3), (3, 2, 2, 0, 2), (3, 2, 2, 1, 2), (3, 0, 3, 0, 3), (3, 0, 3, 1, 3), (3, 0, 3, 0, 2),
    (3, 0, 3, 1, 2), (3, 0, 4, 0, 0), (3, 0, 4, 0, 1), (3, 2, 3, 0, 0), (3, 2, 3, 0, 1), (3, 2, 3, 1, 0),
    (3, 2, 3, 0, 3), (3, 2, 3, 1, 1), (3, 2, 3, 0, 2), (3, 2, 3, 1, 3), (3, 2, 3, 1, 2), (5, 0), (3, 0, 4, 1, 3),
    (3, 0, 4, 1, 2), (3, 2, 4, 0, 0), (3, 2, 4, 0, 1), (3, 2, 4, 1, 3), (3, 2, 4, 1, 2),
)


def flat(value):
    n, rows, width = value.shape
    return value.astype(F32).reshape(n * rows, width).astype(BF16)


def far(side, t):
    return (t < 2) == (side == 0)


def narrow(side, k, t):
    return k >= 3 or (k == 2 and not far(side, t))


def kernel(
    bounds,
    act_hbm, og_hbm, wg_hbm, wu_hbm, wd_hbm,
    gi_ref, gwg_ref, gwu_ref, gwd_ref,
    wg, wu, wd, xbuf, tok, grd, gpart, gsend, grecv,
    w_sem, a_send, a_recv, c_send, c_recv, x_send, x_recv, h_send, h_recv, d_send, d_recv, e_send, e_recv,
    *parts,
):
    row, col = lax.axis_index("row"), lax.axis_index("col")
    y, xh = row // NX, row % NX
    xl, z, core = col // (2 * NZ), (col // 2) % NZ, col % 2
    mine = y * NX + xh
    halves = [parts[7 * h : 7 * h + 7] for h in range(len(bounds))]

    def col_id(dx, dz, dc):
        return (row, ((xl + dx) % 2) * (2 * NZ) + ((z + dz) % NZ) * 2 + (core + dc) % 2)

    def slot_id(slot):
        return col_id(slot // (2 * NZ), (slot // 2) % NZ, slot % 2)

    def slot_there(slot):
        return slot // (2 * NZ) * (2 * NZ) + (NZ - (slot // 2) % NZ) % NZ * 2 + slot % 2

    def row_id(dy, dx):
        return (((y + dy) % NY) * NX + (xh + dx) % NX, col)

    sent = []

    def remote(src, dst, send, recv, device, start=True):
        copy = pltpu.make_async_remote_copy(
            src_ref=src, dst_ref=dst, send_sem=send, recv_sem=recv, device_id=device, device_id_type=MESH
        )
        if start:
            copy.start()
            sent.append(copy)
        return copy

    own = [
        pltpu.make_async_copy(act_hbm, xbuf.at[0, 0], w_sem.at[0]),
        pltpu.make_async_copy(og_hbm, xbuf.at[0, 1], w_sem.at[1]),
    ]
    loads = [
        pltpu.make_async_copy(src, dst, w_sem.at[2 + i])
        for i, (src, dst) in enumerate(((wg_hbm, wg), (wu_hbm, wu), (wd_hbm, wd)))
    ]
    for load in own + loads:
        load.start()

    barrier = pltpu.get_barrier_semaphore()

    def greet(slot, carry):
        pl.semaphore_signal(barrier, inc=1, device_id=slot_id(slot), device_id_type=MESH)
        return carry

    lax.fori_loop(1, 32, greet, 0)
    partners = [row_id(dy, dx) for dy in (0, 1, NY - 1) for dx in range(NX) if dy or dx]
    for partner in partners:
        pl.semaphore_signal(barrier, inc=1, device_id=partner, device_id_type=MESH)
    for load in own:
        load.wait()
    pl.semaphore_wait(barrier, 31 + len(partners))

    def blocks(steps, visit, skip_own=True):
        def body(i, carry):
            step = sum(((i // NX == n) * d for n, d in enumerate(steps)), 0)
            slot = (y + step) % NY * NX + i % NX

            @pl.when(slot != 0)
            def _():
                visit(slot)

            return carry

        lax.fori_loop(0, len(steps) * NX, body, 0)

    def gather(slot, there):
        return pltpu.make_async_remote_copy(
            src_ref=xbuf.at[0], dst_ref=xbuf.at[there], send_sem=a_send.at[there], recv_sem=a_recv.at[there],
            device_id=slot_id(slot), device_id_type=MESH,
        )

    def rows(step):
        return pl.ds((y + step) % NY * NX, NX)

    def stack(values):
        return jnp.concatenate([v.astype(F32).reshape(32, v.shape[2]) for v in values], axis=0).astype(BF16)

    def products(steps):
        blocks(steps, lambda slot: gather(slot, slot).wait_recv())
        here = [xbuf[rows(step)] for step in steps]
        tokens, grads = stack([v[:, 0] for v in here]), stack([v[:, 1] for v in here])
        for (low, high), half in zip(bounds, halves):
            gate = jnp.dot(tokens, wg[:, low:high], preferred_element_type=F32)
            upward = jnp.dot(tokens, wu[:, low:high], preferred_element_type=F32)
            back = lax.dot_general(grads, wd[low:high, :], LAST_DIMS, preferred_element_type=F32)
            for q, value in enumerate((gate, upward, back)):
                for n, step in enumerate(steps):
                    half[0][rows(step), q] = value[32 * n : 32 * n + 32].reshape(NX, 8, high - low)

    blocks(FIRST + LATER, lambda slot: gather(slot_there(slot), slot).start())
    for load in loads:
        load.wait()
    products(FIRST)

    def chain_in(h, side, k, t):
        _, _, in16, _, in32, _, _ = halves[h]
        return in16.at[side, k - 2, t] if narrow(side, k, t) else in32.at[side, k - 1, t]

    def chain(h, side, k, t, start=True):
        _, out16, _, out32, _, _, _ = halves[h]
        out = out16.at[side, k - 2, t] if narrow(side, k, t) else out32.at[side, k - 1, t]
        return remote(
            out, chain_in(h, side, k, t), c_send.at[h, side, k - 1, t], c_recv.at[h, side, k - 1, t],
            row_id(1 if side == 0 else NY - 1, 0), start,
        )

    def hop(h, k, side, t):
        part, out16, _, out32, _, _, _ = halves[h]
        value = part[((y + (k if side == 0 else NY - k)) % NY) * NX + (xh + 1 + t) % NX]
        if k <= 2 or (k == 3 and far(side, t)):
            chain(h, side, k + 1, t, start=False).wait_recv()
            value += chain_in(h, side, k + 1, t)[...].astype(F32)
        if narrow(side, k, t):
            out16[side, k - 2, t] = value.astype(BF16)
        else:
            out32[side, k - 1, t] = value
        chain(h, side, k, t)

    def cross(h, t, there, start=True):
        _, _, _, out32, _, xin, _ = halves[h]
        return remote(
            xin.at[0, t], xin.at[1, t], x_send.at[h, t], x_recv.at[h, t], row_id(0, there), start
        )

    def turn(h, t):
        part, _, _, _, in32, xin, _ = halves[h]
        for side in (0, 1):
            chain(h, side, 1, t, start=False).wait_recv()
        xin[0, t] = in32[0, 0, t] + in32[1, 0, t] + part[y * NX + (xh + 1 + t) % NX]
        if t < NX - 1:
            cross(h, t, 1 + t)

    def share(h, t, block, start=True):
        hbuf = halves[h][6]
        return remote(
            hbuf.at[block], hbuf.at[block], h_send.at[h, t], h_recv.at[h, t], row_id(0, 1 + t), start
        )

    def forward(h, side, k, u, block, start=True):
        hbuf = halves[h][6]
        return remote(
            hbuf.at[block], hbuf.at[block], d_send.at[h, side, k - 1, u], d_recv.at[h, side, k - 1, u],
            row_id(1 if side == 0 else NY - 1, u if k == 1 else 0), start,
        )

    def source(side, k, u):
        return ((y + (NY - k if side == 0 else k)) % NY) * NX + (xh + NX - u) % NX

    def activate(h):
        _, _, _, _, _, xin, hbuf = halves[h]
        for t in (0, 2, 1):
            cross(h, t, 1 + t, start=False).wait_recv()
        sums = xin[0, NX - 1] + xin[1, 0] + xin[1, 1] + xin[1, 2]
        gate, upward, back = sums[0], sums[1], sums[2]
        sigma = jax.nn.sigmoid(gate)
        hbuf[mine, 0] = (gate * sigma * upward).astype(BF16)
        hbuf[mine, 1] = (back * upward * sigma * (1.0 + gate * (1.0 - sigma))).astype(BF16)
        hbuf[mine, 2] = (back * gate * sigma).astype(BF16)
        for side in (0, 1):
            forward(h, side, 1, 0, mine)
        for t in (0, 2, 1):
            share(h, t, mine)
        for u in (1, 3, 2):
            for side in (0, 1):
                forward(h, side, 1, u, mine)

    def spread(h, k, side, u):
        block = source(side, k - 1, u)
        forward(h, side, k - 1, u, block, start=False).wait_recv()
        forward(h, side, k, u, block)

    def returned(slot, there):
        return pltpu.make_async_remote_copy(
            src_ref=gsend.at[slot], dst_ref=grecv.at[there], send_sem=e_send.at[slot], recv_sem=e_recv.at[there],
            device_id=slot_id(slot), device_id_type=MESH,
        )

    def give_back(steps):
        total = None
        for (low, high), half in zip(bounds, halves):
            here = [half[6][rows(step)] for step in steps]
            for q, weight in ((1, wg), (2, wu)):
                term = lax.dot_general(
                    stack([v[:, q] for v in here]), weight[:, low:high], LAST_DIMS, preferred_element_type=F32
                )
                total = term if total is None else total + term
        for n, step in enumerate(steps):
            value = total[32 * n : 32 * n + 32].reshape(NX, 8, total.shape[1])
            gpart[rows(step)] = value
            gsend[rows(step)] = value.astype(BF16)
        blocks(steps, lambda slot: returned(slot, slot_there(slot)).start())

    def nearer():
        for h in range(len(bounds)):
            for t in range(NX - 1):
                share(h, t, source(0, 0, t + 1), start=False).wait_recv()
        give_back(LATER)

    steps = (hop, turn, activate, spread, lambda _: products(LATER), lambda _: nearer())
    for kind, *where in ORDER:
        steps[kind](*where)
    for h in range(len(bounds)):
        for u in (0, 1, 3, 2):
            for side in (0, 1):
                last = 4 if far(side, u) else 3
                forward(h, side, last, u, source(side, last, u), start=False).wait_recv()
    give_back(FIRST)

    tok[...] = flat(xbuf[:, 0])
    grd[...] = flat(xbuf[:, 1])
    for (low, high), half in zip(bounds, halves):
        for out, q in ((gwg_ref, 1), (gwu_ref, 2)):
            out[:, low:high] = lax.dot_general(
                tok[...], flat(half[6][:, q]), FIRST_DIMS, preferred_element_type=F32
            ).astype(BF16)
        gwd_ref[low:high, :] = lax.dot_general(
            flat(half[6][:, 0]), grd[...], FIRST_DIMS, preferred_element_type=F32
        ).astype(BF16)
    for copy in sent:
        copy.wait_send()

    def finish(slot, carry):
        gather(slot, slot).wait_send()
        returned(slot, slot).wait()
        return carry

    lax.fori_loop(1, 32, finish, 0)
    gi_ref[...] = (gpart[0] + jnp.sum(grecv[1:].astype(F32), axis=0)).astype(BF16)


def deliver(*refs):
    sources, targets, sems = refs[:4], refs[4:8], refs[8]
    copies = [pltpu.make_async_copy(s, t, sems.at[i]) for i, (s, t) in enumerate(zip(sources, targets))]
    for copy in copies:
        copy.start()
    for copy in copies:
        copy.wait()


def per_device(activations, out_grad, w_gate, w_up, w_down):
    depth, width = w_gate.shape
    cuts = (0, 384, 640, width)
    bounds = tuple(zip(cuts, cuts[1:]))
    dma = pltpu.SemaphoreType.DMA
    vmem = pl.BlockSpec(memory_space=pltpu.VMEM)
    hbm = pl.BlockSpec(memory_space=pltpu.MemorySpace.HBM)
    shapes = (
        jax.ShapeDtypeStruct((8, depth), BF16),
        jax.ShapeDtypeStruct((depth, width), BF16),
        jax.ShapeDtypeStruct((depth, width), BF16),
        jax.ShapeDtypeStruct((width, depth), BF16),
    )
    parts = []
    for low, high in bounds:
        block = (3, 8, high - low)
        parts += [
            pltpu.VMEM((32,) + block, F32),
            pltpu.VMEM((2, 3, NX) + block, BF16),
            pltpu.VMEM((2, 3, NX) + block, BF16),
            pltpu.VMEM((2, 2, NX) + block, F32),
            pltpu.VMEM((2, 2, NX) + block, F32),
            pltpu.VMEM((2, NX) + block, F32),
            pltpu.VMEM((32,) + block, BF16),
        ]
    n = len(bounds)
    operands = [pltpu.with_memory_space_constraint(x, pltpu.MemorySpace.HBM) for x in (activations, out_grad, w_gate, w_up, w_down)]
    results = pl.pallas_call(
        functools.partial(kernel, bounds),
        out_shape=tuple(pltpu.VMEM(shape.shape, BF16) for shape in shapes),
        in_specs=[hbm] * 5,
        out_specs=(vmem,) * 4,
        scratch_shapes=[
            pltpu.VMEM((depth, width), BF16),
            pltpu.VMEM((depth, width), BF16),
            pltpu.VMEM((width, depth), BF16),
            pltpu.VMEM((32, 2, 8, depth), BF16),
            pltpu.VMEM((256, depth), BF16),
            pltpu.VMEM((256, depth), BF16),
            pltpu.VMEM((32, 8, depth), F32),
            pltpu.VMEM((32, 8, depth), BF16),
            pltpu.VMEM((32, 8, depth), BF16),
            dma((5,)),
            dma((32,)), dma((32,)),
            dma((n, 2, 4, NX)), dma((n, 2, 4, NX)),
            dma((n, NX - 1)), dma((n, NX - 1)),
            dma((n, NX - 1)), dma((n, NX - 1)),
            dma((n, 2, 4, NX)), dma((n, 2, 4, NX)),
            dma((32,)), dma((32,)),
        ] + parts,
        compiler_params=pltpu.CompilerParams(collective_id=0, has_side_effects=True, vmem_limit_bytes=60 << 20),
        name="ffn_backward",
    )(*operands)
    return pl.pallas_call(
        deliver,
        out_shape=shapes,
        in_specs=[vmem] * 4,
        out_specs=(hbm,) * 4,
        scratch_shapes=[dma((4,))],
        compiler_params=pltpu.CompilerParams(vmem_limit_bytes=4 << 20),
        name="deliver",
    )(*results)


def solution(mesh):
    in_specs = (P("col", "row"), P("col", "row"), P("row", "col"), P("row", "col"), P("col", "row"))
    out_specs = (P("col", "row"), P("row", "col"), P("row", "col"), P("col", "row"))
    return jax.shard_map(
        per_device, mesh=mesh, in_specs=in_specs, out_specs=out_specs, check_vma=False
    )
```

```python
import functools

import jax
import jax.numpy as jnp
from jax import lax
from jax.experimental import pallas as pl
from jax.experimental.pallas import tpu as pltpu
from jax.sharding import PartitionSpec as P

MESH = pl.DeviceIdType.MESH
F32 = jnp.float32
BF16 = jnp.bfloat16

NY, NX, NZ = 8, 4, 8
LAST_DIMS = (((1,), (1,)), ((), ()))
FIRST_DIMS = (((0,), (0,)), ((), ()))


ORDER = (
    (0, 0, 4, 0, 1), (0, 0, 3, 1, 1), (0, 1, 4, 0, 1), (0, 0, 3, 0, 3), (0, 0, 4, 1, 2), (0, 0, 4, 0, 0),
    (0, 1, 3, 1, 1), (0, 0, 3, 1, 0), (0, 0, 3, 0, 2), (0, 1, 4, 1, 2), (0, 0, 3, 0, 1), (0, 0, 4, 1, 3),
    (0, 1, 3, 0, 1), (0, 1, 3, 0, 2), (0, 0, 3, 1, 2), (0, 0, 2, 0, 3), (0, 0, 2, 1, 1), (0, 0, 3, 0, 0),
    (0, 1, 3, 1, 0), (0, 0, 2, 0, 2), (0, 1, 3, 1, 2), (0, 0, 2, 1, 0), (0, 0, 2, 0, 1), (0, 1, 4, 1, 3),
    (0, 1, 2, 1, 1), (0, 1, 4, 0, 0), (0, 0, 2, 1, 2), (0, 1, 2, 0, 1), (0, 0, 1, 1, 1), (0, 0, 2, 0, 0),
    (0, 1, 2, 1, 0), (0, 0, 3, 1, 3), (0, 0, 1, 0, 1), (0, 1, 3, 1, 3), (0, 1, 1, 1, 1), (0, 1, 3, 0, 0),
    (0, 0, 1, 1, 2), (0, 1, 2, 1, 2), (0, 0, 1, 0, 2), (0, 1, 1, 0, 1), (0, 1, 2, 0, 2), (1, 0, 1), (0, 0, 1, 1, 0),
    (0, 1, 2, 0, 0), (0, 0, 1, 0, 0), (0, 0, 2, 1, 3), (0, 1, 3, 0, 3), (0, 1, 1, 1, 0), (1, 1, 1), (0, 1, 1, 1, 2),
    (0, 1, 1, 0, 2), (1, 0, 2), (0, 1, 1, 0, 0), (0, 1, 2, 1, 3), (1, 0, 0), (0, 1, 2, 0, 3), (0, 0, 1, 1, 3),
    (0, 0, 1, 0, 3), (1, 1, 0), (1, 1, 2), (0, 1, 1, 0, 3), (0, 1, 1, 1, 3), (1, 0, 3), (2, 0), (1, 1, 3), (2, 1),
    (3, 0, 2, 1, 0), (3, 0, 2, 0, 0), (3, 0, 1, 1, 3), (3, 0, 1, 0, 1), (3, 0, 1, 1, 1), (3, 0, 1, 0, 3),
    (3, 1, 2, 1, 0), (3, 0, 1, 0, 2), (3, 0, 1, 1, 2), (3, 1, 1, 0, 3), (3, 1, 1, 0, 1), (3, 1, 1, 1, 1),
    (3, 1, 1, 1, 3), (3, 0, 2, 1, 3), (3, 0, 2, 0, 1), (3, 1, 1, 1, 2), (3, 1, 1, 0, 2), (3, 0, 2, 0, 3),
    (3, 1, 2, 0, 0), (3, 0, 2, 1, 1), (3, 0, 3, 0, 0), (3, 0, 2, 1, 2), (3, 1, 2, 0, 3), (3, 1, 2, 0, 1),
    (3, 1, 2, 1, 3), (3, 1, 2, 1, 1), (3, 0, 3, 1, 3), (3, 0, 2, 0, 2), (3, 0, 3, 0, 1), (3, 1, 2, 1, 2),
    (3, 1, 3, 0, 0), (3, 0, 3, 1, 1), (3, 1, 2, 0, 2), (3, 1, 3, 1, 3), (3, 1, 3, 0, 3), (3, 0, 3, 1, 2),
    (3, 1, 3, 1, 0), (3, 1, 3, 0, 1), (3, 0, 4, 0, 0), (3, 1, 3, 1, 1), (3, 1, 3, 1, 2), (3, 0, 4, 0, 1),
    (3, 0, 4, 1, 3), (3, 0, 3, 0, 2), (3, 1, 4, 0, 0), (3, 0, 3, 1, 0), (3, 1, 4, 1, 3), (3, 0, 3, 0, 3),
    (3, 0, 4, 1, 2), (3, 1, 4, 0, 1), (3, 1, 3, 0, 2), (3, 1, 4, 1, 2),
)


def flat(value):
    n, rows, width = value.shape
    return value.astype(F32).reshape(n * rows, width).astype(BF16)


def far(side, t):
    return (t < 2) == (side == 0)


def narrow(side, k, t):
    return k >= 3 or (k == 2 and not far(side, t))


def kernel(
    bounds,
    act_hbm, og_hbm, wg_hbm, wu_hbm, wd_hbm,
    gi_ref, gwg_ref, gwu_ref, gwd_ref,
    wg, wu, wd, xbuf, tok, grd, gpart, gsend, grecv,
    w_sem, a_send, a_recv, c_send, c_recv, x_send, x_recv, h_send, h_recv, d_send, d_recv, e_send, e_recv,
    *parts,
):
    row, col = lax.axis_index("row"), lax.axis_index("col")
    y, xh = row >> 2, row & 3
    xl, z, core = col >> 4, (col >> 1) & 7, col & 1
    mine = row
    ys, xs = [((y + dy) & 7) << 2 for dy in range(NY)], [(xh + dx) & 3 for dx in range(NX)]
    blocks_at = [[yy + xx for xx in xs] for yy in ys]
    halves = [parts[7 * h : 7 * h + 7] for h in range(len(bounds))]

    def col_id(dx, dz, dc):
        return (row, (((xl + dx) & 1) << 4) + (((z + dz) & 7) << 1) + ((core + dc) & 1))

    def slot_id(slot):
        return col_id(slot >> 4, (slot >> 1) & 7, slot & 1)

    def slot_there(slot):
        return (slot & 17) + (((NZ - ((slot >> 1) & 7)) & 7) << 1)

    def row_id(dy, dx):
        return (blocks_at[dy % NY][dx % NX], col)

    sent = []

    def remote(src, dst, send, recv, device, start=True):
        copy = pltpu.make_async_remote_copy(
            src_ref=src, dst_ref=dst, send_sem=send, recv_sem=recv, device_id=device, device_id_type=MESH
        )
        if start:
            copy.start()
            sent.append(copy)
        return copy

    own = [
        pltpu.make_async_copy(act_hbm, xbuf.at[0, 0], w_sem.at[0]),
        pltpu.make_async_copy(og_hbm, xbuf.at[0, 1], w_sem.at[1]),
    ]
    loads = [
        pltpu.make_async_copy(src, dst, w_sem.at[2 + i])
        for i, (src, dst) in enumerate(((wg_hbm, wg), (wu_hbm, wu), (wd_hbm, wd)))
    ]
    for load in own + loads:
        load.start()

    barrier = pltpu.get_barrier_semaphore()

    def greet(slot, carry):
        pl.semaphore_signal(barrier, inc=1, device_id=slot_id(slot), device_id_type=MESH)
        return carry

    lax.fori_loop(1, 32, greet, 0)
    partners = [row_id(1, 0), row_id(NY - 1, 0)] + [row_id(0, dx) for dx in range(1, NX)]
    for partner in partners:
        pl.semaphore_signal(barrier, inc=1, device_id=partner, device_id_type=MESH)
    for load in own:
        load.wait()
    pl.semaphore_wait(barrier, 31 + len(partners))

    def gather(slot, there, device, start=True):
        return remote(xbuf.at[slot], xbuf.at[there], a_send.at[there], a_recv.at[there], device, start)

    order = [dx * 2 * NZ + dz * 2 for dz in (0, 1, 7, 2, 6, 3, 5, 4) for dx in (0, 1)]
    for slot in order[1:]:
        gather(0, slot_there(slot), slot_id(slot))
    for slot in order:
        if slot > 0:
            gather(slot, slot, slot_id(1), start=False).wait_recv()
        gather(slot, slot + 1, slot_id(1))
    for slot in order:
        gather(slot + 1, slot + 1, slot_id(1), start=False).wait_recv()
    tok[...] = flat(xbuf[:, 0])
    grd[...] = flat(xbuf[:, 1])
    for load in loads:
        load.wait()

    def products(h):
        low, high = bounds[h]
        part = halves[h][0]
        part[:, 0] = jnp.dot(tok[...], wg[:, low:high], preferred_element_type=F32).reshape(32, 8, high - low)
        part[:, 1] = jnp.dot(tok[...], wu[:, low:high], preferred_element_type=F32).reshape(32, 8, high - low)
        part[:, 2] = lax.dot_general(
            grd[...], wd[low:high, :], LAST_DIMS, preferred_element_type=F32
        ).reshape(32, 8, high - low)

    def chain_in(h, side, k, t):
        _, _, in16, _, in32, _, _ = halves[h]
        return in16.at[side, k - 2, t] if narrow(side, k, t) else in32.at[side, k - 1, t]

    def chain(h, side, k, t, start=True):
        _, out16, _, out32, _, _, _ = halves[h]
        out = out16.at[side, k - 2, t] if narrow(side, k, t) else out32.at[side, k - 1, t]
        return remote(
            out, chain_in(h, side, k, t), c_send.at[h, side, k - 1, t], c_recv.at[h, side, k - 1, t],
            row_id(1 if side == 0 else NY - 1, 0), start,
        )

    def hop(h, k, side, t):
        part, out16, _, out32, _, _, _ = halves[h]
        value = part[blocks_at[(k if side == 0 else NY - k) % NY][(1 + t) % NX]]
        if k <= 2 or (k == 3 and far(side, t)):
            chain(h, side, k + 1, t, start=False).wait_recv()
            value += chain_in(h, side, k + 1, t)[...].astype(F32)
        if narrow(side, k, t):
            out16[side, k - 2, t] = value.astype(BF16)
        else:
            out32[side, k - 1, t] = value
        chain(h, side, k, t)

    def cross(h, t, there, start=True):
        _, _, _, out32, _, xin, _ = halves[h]
        return remote(
            xin.at[0, t], xin.at[1, t], x_send.at[h, t], x_recv.at[h, t], row_id(0, there), start
        )

    def turn(h, t):
        part, _, _, _, in32, xin, _ = halves[h]
        for side in (0, 1):
            chain(h, side, 1, t, start=False).wait_recv()
        xin[0, t] = in32[0, 0, t] + in32[1, 0, t] + part[blocks_at[0][(1 + t) % NX]]
        if t < NX - 1:
            cross(h, t, 1 + t)

    def share(h, t, block, start=True):
        hbuf = halves[h][6]
        return remote(
            hbuf.at[block], hbuf.at[block], h_send.at[h, t], h_recv.at[h, t], row_id(0, 1 + t), start
        )

    def forward(h, side, k, u, block, start=True):
        hbuf = halves[h][6]
        return remote(
            hbuf.at[block], hbuf.at[block], d_send.at[h, side, k - 1, u], d_recv.at[h, side, k - 1, u],
            row_id(1 if side == 0 else NY - 1, 0), start,
        )

    def source(side, k, u):
        return blocks_at[(NY - k if side == 0 else k) % NY][(NX - u) % NX]

    def activate(h):
        _, _, _, _, _, xin, hbuf = halves[h]
        for t in (0, 2, 1):
            cross(h, t, 1 + t, start=False).wait_recv()
        sums = xin[0, NX - 1] + xin[1, 0] + xin[1, 1] + xin[1, 2]
        gate, upward, back = sums[0], sums[1], sums[2]
        sigma = jax.nn.sigmoid(gate)
        hbuf[mine, 0] = (gate * sigma * upward).astype(BF16)
        hbuf[mine, 1] = (back * upward * sigma * (1.0 + gate * (1.0 - sigma))).astype(BF16)
        hbuf[mine, 2] = (back * gate * sigma).astype(BF16)
        for side in (0, 1):
            forward(h, side, 1, 0, mine)
        for t in (0, 2, 1):
            share(h, t, mine)

    shared = set()

    def spread(h, k, side, u):
        block = source(side, k - 1, u)
        if k > 1:
            forward(h, side, k - 1, u, block, start=False).wait_recv()
        elif (h, u) not in shared:
            shared.add((h, u))
            share(h, u - 1, block, start=False).wait_recv()
        forward(h, side, k, u, block)

    def landed(h):
        for u in (0, 1, 3, 2):
            for side in (0, 1):
                last = 4 if far(side, u) else 3
                forward(h, side, last, u, source(side, last, u), start=False).wait_recv()

    steps = (hop, turn, activate, spread)
    ready = set()
    for kind, h, *where in ORDER:
        if h not in ready:
            ready.add(h)
            products(h)
        steps[kind](h, *where)
    landed(0)
    landed(1)

    grads = [(flat(half[6][:, 1]), flat(half[6][:, 2])) for half in halves]
    total = None
    for (low, high), (grad_gate, grad_up) in zip(bounds, grads):
        for grad, weight in ((grad_gate, wg), (grad_up, wu)):
            term = lax.dot_general(grad, weight[:, low:high], LAST_DIMS, preferred_element_type=F32)
            total = term if total is None else total + term
    gpart[...] = total.reshape(32, 8, total.shape[1])
    gsend[...] = gpart[...].astype(BF16)

    def returned(slot, there, device):
        return pltpu.make_async_remote_copy(
            src_ref=gsend.at[slot], dst_ref=grecv.at[there], send_sem=e_send.at[slot], recv_sem=e_recv.at[there],
            device_id=device, device_id_type=MESH,
        )

    def return_start(slot, carry):
        returned(slot, slot_there(slot), slot_id(slot)).start()
        return carry

    lax.fori_loop(1, 32, return_start, 0)
    for (low, high), half, (grad_gate, grad_up) in zip(bounds, halves, grads):
        for out, grad in ((gwg_ref, grad_gate), (gwu_ref, grad_up)):
            out[:, low:high] = lax.dot_general(
                tok[...], grad, FIRST_DIMS, preferred_element_type=F32
            ).astype(BF16)
        gwd_ref[low:high, :] = lax.dot_general(
            flat(half[6][:, 0]), grd[...], FIRST_DIMS, preferred_element_type=F32
        ).astype(BF16)
    for copy in sent:
        copy.wait_send()

    def return_wait(slot, carry):
        returned(slot, slot, slot_id(slot)).wait()
        return carry

    lax.fori_loop(1, 32, return_wait, 0)
    gi_ref[...] = (gpart[0] + jnp.sum(grecv[1:].astype(F32), axis=0)).astype(BF16)


def deliver(*refs):
    sources, targets, sems = refs[:4], refs[4:8], refs[8]
    copies = [pltpu.make_async_copy(s, t, sems.at[i]) for i, (s, t) in enumerate(zip(sources, targets))]
    for copy in copies:
        copy.start()
    for copy in copies:
        copy.wait()


def per_device(activations, out_grad, w_gate, w_up, w_down):
    depth, width = w_gate.shape
    cut = (width // 128 + 1) // 2 * 128
    bounds = ((0, cut), (cut, width))
    dma = pltpu.SemaphoreType.DMA
    vmem = pl.BlockSpec(memory_space=pltpu.VMEM)
    hbm = pl.BlockSpec(memory_space=pltpu.MemorySpace.HBM)
    shapes = (
        jax.ShapeDtypeStruct((8, depth), BF16),
        jax.ShapeDtypeStruct((depth, width), BF16),
        jax.ShapeDtypeStruct((depth, width), BF16),
        jax.ShapeDtypeStruct((width, depth), BF16),
    )
    parts = []
    for low, high in bounds:
        block = (3, 8, high - low)
        parts += [
            pltpu.VMEM((32,) + block, F32),
            pltpu.VMEM((2, 3, NX) + block, BF16),
            pltpu.VMEM((2, 3, NX) + block, BF16),
            pltpu.VMEM((2, 2, NX) + block, F32),
            pltpu.VMEM((2, 2, NX) + block, F32),
            pltpu.VMEM((2, NX) + block, F32),
            pltpu.VMEM((32,) + block, BF16),
        ]
    n = len(bounds)
    operands = [pltpu.with_memory_space_constraint(x, pltpu.MemorySpace.HBM) for x in (activations, out_grad, w_gate, w_up, w_down)]
    results = pl.pallas_call(
        functools.partial(kernel, bounds),
        out_shape=tuple(pltpu.VMEM(shape.shape, BF16) for shape in shapes),
        in_specs=[hbm] * 5,
        out_specs=(vmem,) * 4,
        scratch_shapes=[
            pltpu.VMEM((depth, width), BF16),
            pltpu.VMEM((depth, width), BF16),
            pltpu.VMEM((width, depth), BF16),
            pltpu.VMEM((32, 2, 8, depth), BF16),
            pltpu.VMEM((256, depth), BF16),
            pltpu.VMEM((256, depth), BF16),
            pltpu.VMEM((32, 8, depth), F32),
            pltpu.VMEM((32, 8, depth), BF16),
            pltpu.VMEM((32, 8, depth), BF16),
            dma((5,)),
            dma((32,)), dma((32,)),
            dma((n, 2, 4, NX)), dma((n, 2, 4, NX)),
            dma((n, NX - 1)), dma((n, NX - 1)),
            dma((n, NX - 1)), dma((n, NX - 1)),
            dma((n, 2, 4, NX)), dma((n, 2, 4, NX)),
            dma((32,)), dma((32,)),
        ] + parts,
        compiler_params=pltpu.CompilerParams(collective_id=0, has_side_effects=True, vmem_limit_bytes=60 << 20),
        name="ffn_backward",
    )(*operands)
    return pl.pallas_call(
        deliver,
        out_shape=shapes,
        in_specs=[vmem] * 4,
        out_specs=(hbm,) * 4,
        scratch_shapes=[dma((4,))],
        compiler_params=pltpu.CompilerParams(vmem_limit_bytes=4 << 20),
        name="deliver",
    )(*results)


def solution(mesh):
    in_specs = (P("col", "row"), P("col", "row"), P("row", "col"), P("row", "col"), P("col", "row"))
    out_specs = (P("col", "row"), P("row", "col"), P("row", "col"), P("col", "row"))
    return jax.shard_map(
        per_device, mesh=mesh, in_specs=in_specs, out_specs=out_specs, check_vma=False
    )
```
